32 devices in a mesh: gx: 4 (over y, x), gy: 8 (over z, core).
Axes of the slice: x: 2, y: 2, z: 4, core: 2. Of those that a mesh axis runs over, the one named last changes fastest.
Arguments:
- vertex_state: bfloat16 [256, 256, 128], P(('gx', 'gy')), may hold values from -6 to 6
- edge_state: bfloat16 [256, 1536, 128], P(('gx', 'gy')), may hold values from -6 to 6
- senders: int32 [256, 1536], P(('gx', 'gy')), may hold values from 0 to 511
- receivers: int32 [256, 1536], P(('gx', 'gy')), may hold values from 0 to 255
- counts: int32 [256], P(('gx', 'gy')), may hold values from 768 to 1536
- border_rows: int32 [256, 2, 128], P(('gx', 'gy')), may hold values from 0 to 255
- old_neighbours: int32 [256, 2], P(('gx', 'gy')), may hold values from 0 to 255, as said below
- new_neighbours: int32 [256, 2], P(('gx', 'gy')), may hold values from 0 to 255, as said below
- new_place: int32 [256], P(('gx', 'gy')), may hold values from 0 to 255, as said below
- weights_in: bfloat16 [3, 5, 128, 128], replicated, may hold values from -0.5 to 0.5
- weights_out: bfloat16 [3, 2, 128, 128], replicated, may hold values from -0.5 to 0.5
- biases: float32 [3, 6, 128], replicated, may hold values from -3 to 3
- norm_gains: float32 [3, 2, 128], replicated, may hold values from 0.25 to 1.75
Outputs:
- vertex_out: bfloat16 [256, 256, 128], P(('gx', 'gy'))
- edge_out: bfloat16 [256, 1536, 128], P(('gx', 'gy'))
The draws below stay inside these ranges and needn't reach their ends.
Inputs may be any that keep to these rules, and one draw needn't show every extreme that they name: A permutation of the patches. With devices numbered gx-index times the size of gy plus gy-index, patch p stands on device p // 8 and moves to device new_place[p] // 8, which has the same gx-index; one device sends at most 1 patch to any one device, and some pair of devices reaches 1. old_neighbours[p, 0] stands on the device whose gy-index is one less than that of p's device (cyclically) and whose gx-index is the same; old_neighbours[p, 1] on the device whose gx-index is one less (cyclically) and whose gy-index is the same. new_neighbours[new_place[p], k] = new_place[old_neighbours[p, k]]; in the new positions it follows the same rule as old_neighbours.
All inputs are finite; a program needn't handle non-finite values.
Results may differ from the reference program's by a relative error of at most 0.0066.
Values may be sent and summed in bfloat16 or wider, within the bound.
A program may use at most 128 MiB of HBM per device.

```python
import jax
import jax.numpy as jnp
from jax import lax

WIDTH = 128
VERTS = 256
EDGES = 1536
BORDER = 128
PATCH_DEV = 8
STEPS_OLD = 2
STEPS_NEW = 1
STEPS = 3
PATCHES = 256
N_GX = 4
N_GY = 8


def patch_layout(key):
    seed_base = jax.random.fold_in(key, 4242)
    shift_key, old_key, new_key = jax.random.split(seed_base, 3)
    capacity = (PATCH_DEV + N_GY - 1) // N_GY
    raw_offsets = (jax.random.permutation(shift_key, N_GY * capacity)[:PATCH_DEV] // capacity).astype(jnp.int32)
    offsets = ((raw_offsets - raw_offsets[0] + N_GY // 2) % N_GY).astype(jnp.int32)
    device_total = N_GX * N_GY
    old_slots = jax.vmap(lambda sub_key: jax.random.permutation(sub_key, PATCH_DEV))(jax.random.split(old_key, device_total)).reshape(N_GX, N_GY, PATCH_DEV).astype(jnp.int32)
    new_slots = jax.vmap(lambda sub_key: jax.random.permutation(sub_key, PATCH_DEV))(jax.random.split(new_key, device_total)).reshape(N_GX, N_GY, PATCH_DEV).astype(jnp.int32)
    along_x = jnp.arange(N_GX, dtype=jnp.int32)[:, None, None]
    along_y = jnp.arange(N_GY, dtype=jnp.int32)[None, :, None]
    tracks = jnp.arange(PATCH_DEV, dtype=jnp.int32)[None, None, :]

    def old_position(row_x, row_y):
        row_x = row_x % N_GX
        row_y = row_y % N_GY
        return (row_x * N_GY + row_y) * PATCH_DEV + old_slots[row_x, row_y, tracks]

    def new_position(row_x, row_y):
        row_x = row_x % N_GX
        landing = (row_y + offsets[tracks]) % N_GY
        return (row_x * N_GY + landing) * PATCH_DEV + new_slots[row_x, landing, tracks]
    old_spots = old_position(along_x, along_y).reshape(-1)
    new_spots = new_position(along_x, along_y).reshape(-1)
    patch_total = device_total * PATCH_DEV
    place_table = jnp.zeros((patch_total,), jnp.int32).at[old_spots].set(new_spots)
    old_links = jnp.stack([old_position(along_x, along_y - 1), old_position(along_x - 1, along_y)], axis=-1).reshape(-1, 2)
    new_links = jnp.stack([new_position(along_x, along_y - 1), new_position(along_x - 1, along_y)], axis=-1).reshape(-1, 2)
    old_table = jnp.zeros((patch_total, 2), jnp.int32).at[old_spots].set(old_links)
    new_table = jnp.zeros((patch_total, 2), jnp.int32).at[new_spots].set(new_links)
    return (place_table, old_table, new_table)


def draw_new_place(key, part):
    return patch_layout(key)[0]


def draw_old_neighbours(key, part):
    return patch_layout(key)[1]


def draw_new_neighbours(key, part):
    return patch_layout(key)[2]


def touch_ends(entries, key, least, largest):
    longest = entries.shape.index(max(entries.shape))
    spots = []
    for shift in (0, 1):
        where = [jax.random.randint(jax.random.fold_in(key, axis), (), 0, length) for axis, length in enumerate(entries.shape)]
        where[longest] = (where[longest] + shift) % entries.shape[longest]
        spots.append(tuple(where))
    return entries.at[spots[0]].set(least).at[spots[1]].set(largest)


def block_scale(stream_key, dims, cuts, least, top_value):
    def one(position, blocks):
        steps = jax.random.uniform(jax.random.fold_in(jax.random.fold_in(stream_key, 6), position), (blocks,), jnp.float32, least / len(cuts), top_value / len(cuts))
        return jnp.repeat(jnp.exp(steps), dims[position] // blocks).reshape((-1,) + (1,) * (len(dims) - position - 1))

    gain = one(*cuts[0])
    for cut in cuts[1:]:
        gain = gain * one(*cut)
    return gain


def noise(key, shape, scale, most, cuts=(), held_as=jnp.bfloat16):
    loudness = block_scale(key, shape, cuts, -0.22, 0.18) if cuts else 1.0
    values = jax.random.normal(key, shape, jnp.float32) * scale * loudness
    return jnp.minimum(jnp.maximum(values, -most), most).astype(held_as)


def setup_inputs(seed: int = 0) -> dict:
    key_of = jax.random.split(jax.random.key(seed), 14)
    return {
        "vertex_state": noise(key_of[0], (PATCHES, VERTS, WIDTH), 1.0, 6.0, ((0, 32),)),
        "edge_state": noise(key_of[1], (PATCHES, EDGES, WIDTH), 1.0, 6.0, ((0, 32),)),
        "senders": touch_ends(jax.random.randint(key_of[2], (PATCHES, EDGES), 0, VERTS + 2 * BORDER), jax.random.fold_in(key_of[2], 1), 0, (VERTS + 2 * BORDER) - 1).astype(jnp.int32),
        "receivers": touch_ends(jax.random.randint(key_of[3], (PATCHES, EDGES), 0, VERTS), jax.random.fold_in(key_of[3], 1), 0, VERTS - 1).astype(jnp.int32),
        "counts": touch_ends(jax.random.randint(key_of[4], (PATCHES,), EDGES // 2, EDGES + 1), jax.random.fold_in(key_of[4], 1), EDGES // 2, EDGES).astype(jnp.int32),
        "border_rows": touch_ends(jax.random.randint(key_of[5], (PATCHES, 2, BORDER), 0, VERTS), jax.random.fold_in(key_of[5], 1), 0, VERTS - 1).astype(jnp.int32),
        "old_neighbours": draw_old_neighbours(jax.random.fold_in(key_of[13], 71), 0),
        "new_neighbours": draw_new_neighbours(jax.random.fold_in(key_of[13], 71), 0),
        "new_place": draw_new_place(jax.random.fold_in(key_of[13], 71), 0),
        "weights_in": noise(key_of[9], (STEPS, 5, WIDTH, WIDTH), WIDTH ** -0.5, 0.5),
        "weights_out": noise(key_of[10], (STEPS, 2, WIDTH, WIDTH), WIDTH ** -0.5, 0.5),
        "biases": noise(key_of[11], (STEPS, 6, WIDTH), 0.5, 3.0, (), jnp.float32),
        "norm_gains": jnp.clip(1.0 + 0.15 * jax.random.normal(key_of[12], (STEPS, 2, WIDTH), jnp.float32), 0.25, 1.75),
    }


def product(left, right):
    return jnp.dot(left, right, preferred_element_type=jnp.float32)

def normalize(values, scale_row, shift_row):
    center = values - lax.optimization_barrier(jnp.mean(values, axis=-1, keepdims=True))
    spread = lax.optimization_barrier(jnp.mean(center * center, axis=-1, keepdims=True))
    return center * lax.rsqrt(spread + 1e-05) * scale_row + shift_row

def ghost_rows(vertex_state, border_rows, neighbours):
    patch_rows = jnp.arange(vertex_state.shape[0], dtype=jnp.int32)[:, None]
    along_gy = vertex_state[patch_rows, border_rows[:, 0]]
    along_gx = vertex_state[patch_rows, border_rows[:, 1]]
    return jnp.concatenate([along_gy[neighbours[:, 0]], along_gx[neighbours[:, 1]]], axis=1)

def patch_update(layer_weights, pieces):
    weights_in, weights_out, bias_rows, gain_rows = layer_weights
    vertex_block, ghost_block, edge_block, sender_ids, receiver_ids, edge_count = pieces
    vertex_count = vertex_block.shape[0]
    edge_total = edge_block.shape[0]
    joined = jnp.concatenate([vertex_block, ghost_block], axis=0)
    sender_terms = product(joined, weights_in[1]).astype(jnp.bfloat16)
    receiver_terms = product(vertex_block, weights_in[2]).astype(jnp.bfloat16)
    summed = product(edge_block, weights_in[0]) + sender_terms[sender_ids].astype(jnp.float32)
    summed = summed + receiver_terms[receiver_ids].astype(jnp.float32) + bias_rows[0]
    edge_hidden = jax.nn.relu(summed).astype(jnp.bfloat16)
    edge_update = normalize(product(edge_hidden, weights_out[0]) + bias_rows[1], gain_rows[0], bias_rows[2])
    live = jnp.arange(edge_total, dtype=jnp.int32) < edge_count
    widened = edge_block.astype(jnp.float32)
    fresh_edges = jnp.where(live[:, None], widened + edge_update, widened).astype(jnp.bfloat16)
    masked = jnp.where(live[:, None], fresh_edges.astype(jnp.float32), jnp.zeros_like(widened))
    aggregate = jax.ops.segment_sum(masked, receiver_ids, num_segments=vertex_count).astype(jnp.bfloat16)
    node_hidden = product(vertex_block, weights_in[3]) + product(aggregate, weights_in[4]) + bias_rows[3]
    node_hidden = jax.nn.relu(node_hidden).astype(jnp.bfloat16)
    vertex_update = normalize(product(node_hidden, weights_out[1]) + bias_rows[4], gain_rows[1], bias_rows[5])
    fresh_vertices = (vertex_block.astype(jnp.float32) + vertex_update).astype(jnp.bfloat16)
    return (fresh_vertices, fresh_edges)

def full_step(layer_weights, vertex_state, edge_state, senders, receivers, counts, border_rows, neighbours):
    ghosts = ghost_rows(vertex_state, border_rows, neighbours)
    return lax.map(lambda pieces: patch_update(layer_weights, pieces), (vertex_state, ghosts, edge_state, senders, receivers, counts))

def relocate(values, new_place):
    return jnp.zeros_like(values).at[new_place].set(values)

def reference(vertex_state, edge_state, senders, receivers, counts, border_rows, old_neighbours, new_neighbours, new_place, weights_in, weights_out, biases, norm_gains):
    for step_index in range(STEPS_OLD):
        layer_weights = (weights_in[step_index], weights_out[step_index], biases[step_index], norm_gains[step_index])
        vertex_state, edge_state = full_step(layer_weights, vertex_state, edge_state, senders, receivers, counts, border_rows, old_neighbours)
    vertex_state = relocate(vertex_state, new_place)
    edge_state = relocate(edge_state, new_place)
    senders = relocate(senders, new_place)
    receivers = relocate(receivers, new_place)
    counts = relocate(counts, new_place)
    border_rows = relocate(border_rows, new_place)
    for step_index in range(STEPS_NEW):
        which = STEPS_OLD + step_index
        layer_weights = (weights_in[which], weights_out[which], biases[which], norm_gains[which])
        vertex_state, edge_state = full_step(layer_weights, vertex_state, edge_state, senders, receivers, counts, border_rows, new_neighbours)
    return (vertex_state, edge_state)
```

```python
import functools

import jax
import jax.numpy as jnp
from jax import lax
from jax.experimental import pallas as pl
from jax.experimental.pallas import tpu as pltpu
from jax.sharding import PartitionSpec as P

CHUNK = 256
BF = jnp.bfloat16
F32 = jnp.float32


def product(left, right):
    return jnp.dot(left, right, preferred_element_type=F32)


def normalize(values, scale_row, shift_row):
    center = values - jnp.mean(values, axis=-1, keepdims=True)
    spread = jnp.mean(center * center, axis=-1, keepdims=True)
    return center * lax.rsqrt(spread + 1e-05) * scale_row + shift_row


def ones_where(mask):
    return jnp.where(mask, jnp.ones((), BF), jnp.zeros((), BF))


def spread_ids(row):
    return jnp.transpose(jnp.broadcast_to(row, (128, row.shape[1])))


def one_hot(wide, number, first=0):
    lanes = lax.broadcasted_iota(jnp.int32, wide.shape, 1)
    parts = [
        ones_where(wide == (lanes + (first + start)).astype(F32).astype(BF))
        for start in range(0, number, 128)
    ]
    return jnp.concatenate(parts, axis=1)


def pick_borders(border_ids, vertices):
    wide = spread_ids(border_ids.astype(F32).astype(BF))
    return product(one_hot(wide, vertices.shape[0]), vertices).astype(BF)


def border_kernel(order, v_ref, b_ref, out_ref):
    out_ref[0] = pick_borders(b_ref[0], v_ref[0])


def step_kernel(last, inp, ids, outs, counts, v_ref, e_ref, s_ref, r_ref, b_ref, gy_ref, gx_ref,
                win, wout, bias, gain, *rest):
    if last:
        vo_ref, eo_ref, terms, agg = rest[-4:]
    else:
        vo_ref, eo_ref, bo_ref, terms, agg = rest
    verts = v_ref.shape[1]
    edges = e_ref.shape[1]
    border = gy_ref.shape[1]
    senders_all = verts + 2 * border
    vertices = v_ref[0]
    terms[pl.ds(0, verts)] = product(vertices, win[1]).astype(BF)
    terms[pl.ds(verts, border)] = product(gy_ref[0], win[1]).astype(BF)
    terms[pl.ds(verts + border, border)] = product(gx_ref[0], win[1]).astype(BF)
    terms[pl.ds(senders_all, verts)] = product(vertices, win[2]).astype(BF)
    agg[...] = jnp.zeros_like(agg)
    count = counts[pl.program_id(0)]
    half = senders_all // 2

    def chunk(c, carry):
        base = pl.multiple_of(c * CHUNK, CHUNK)
        rows = pl.ds(base, CHUNK)
        edge = e_ref[0, rows, :]
        sent = (s_ref[0, :, rows] - half).astype(F32).astype(BF)
        lane = base + lax.broadcasted_iota(jnp.int32, (1, CHUNK), 1)
        recv = jnp.where(lane < count, r_ref[0, :, rows], -1).astype(F32).astype(BF)
        hot_s = one_hot(spread_ids(sent), senders_all, -half)
        hot_r = one_hot(spread_ids(recv), verts)
        summed = (
            product(edge, win[0])
            + product(jnp.concatenate([hot_s, hot_r], axis=1), terms[...])
            + bias[0:1, :]
        )
        hidden = jnp.maximum(summed, 0.0).astype(BF)
        update = normalize(product(hidden, wout[0]) + bias[1:2, :], gain[0:1, :], bias[2:3, :])
        row = base + lax.broadcasted_iota(jnp.int32, edge.shape, 0)
        widened = edge.astype(F32)
        fresh = jnp.where(row < count, widened + update, widened).astype(BF)
        eo_ref[0, rows, :] = fresh
        tall = lax.broadcasted_iota(jnp.int32, (verts, CHUNK), 0).astype(F32).astype(BF)
        incoming = ones_where(tall == recv)
        agg[...] += product(incoming, fresh)
        return carry

    live_chunks = (count + (CHUNK - 1)) // CHUNK
    lax.fori_loop(0, live_chunks, chunk, 0)

    def keep(c, carry):
        rows = pl.ds(pl.multiple_of(c * CHUNK, CHUNK), CHUNK)
        eo_ref[0, rows, :] = e_ref[0, rows, :]
        return carry

    lax.fori_loop(live_chunks, edges // CHUNK, keep, 0)

    hidden = product(vertices, win[3]) + product(agg[...].astype(BF), win[4]) + bias[3:4, :]
    hidden = jnp.maximum(hidden, 0.0).astype(BF)
    update = normalize(product(hidden, wout[1]) + bias[4:5, :], gain[1:2, :], bias[5:6, :])
    fresh = (vertices.astype(F32) + update).astype(BF)
    vo_ref[0] = fresh
    if not last:
        bo_ref[0] = pick_borders(b_ref[0], fresh)


def run_borders(order, vertex_state, border_ids):
    patches, verts, width = vertex_state.shape
    wanted = border_ids.shape[2]
    return pl.pallas_call(
        border_kernel,
        out_shape=jax.ShapeDtypeStruct((patches, wanted, width), BF),
        grid_spec=pltpu.PrefetchScalarGridSpec(
            num_scalar_prefetch=1,
            grid=(patches,),
            in_specs=[
                pl.BlockSpec((1, verts, width), lambda p, o: (o[p], 0, 0)),
                pl.BlockSpec((1, 1, wanted), lambda p, o: (o[p], 0, 0)),
            ],
            out_specs=pl.BlockSpec((1, wanted, width), lambda p, o: (p, 0, 0)),
        ),
        cost_estimate=pl.CostEstimate(flops=10**9, bytes_accessed=10**6, transcendentals=0),
    )(order, vertex_state, border_ids)


def run_step(weights, inp, ids, outs, counts, v, e, lists, gy_rows, gx_rows, patches, finals=None):
    senders, receivers, border_ids = lists
    win, wout, bias, gain = weights
    number = counts.shape[0]
    verts, width = v.shape[1:]
    edges = e.shape[1]
    wanted = border_ids.shape[2]
    last = finals is not None

    def at(which):
        return lambda p, *tables: (tables[which][p], 0, 0)

    def own(p, *tables):
        return (p, 0, 0)

    def whole(array):
        return pl.BlockSpec(array.shape, lambda p, *tables: (0,) * array.ndim)

    in_specs = [
        pl.BlockSpec((1, verts, width), at(0)),
        pl.BlockSpec((1, edges, width), at(0)),
        pl.BlockSpec((1, 1, edges), at(1)),
        pl.BlockSpec((1, 1, edges), at(1)),
        pl.BlockSpec((1, 1, wanted), at(1)),
        pl.BlockSpec((1,) + gy_rows.shape[1:], own),
        pl.BlockSpec((1,) + gx_rows.shape[1:], own),
        whole(win), whole(wout), whole(bias), whole(gain),
    ]
    operands = [v, e, senders, receivers, border_ids, gy_rows, gx_rows, win, wout, bias, gain]
    out_specs = [pl.BlockSpec((1, verts, width), at(2)), pl.BlockSpec((1, edges, width), at(2))]
    if last:
        in_specs += [pl.BlockSpec(memory_space=pl.ANY)] * len(finals)
        operands += list(finals)
        shapes = [
            jax.ShapeDtypeStruct((patches, verts, width), BF),
            jax.ShapeDtypeStruct((patches, edges, width), BF),
        ]
        aliases = {4 + 11: 0, 4 + 12: 1} if finals else {}
    else:
        out_specs.append(pl.BlockSpec((1, wanted, width), own))
        shapes = [
            jax.ShapeDtypeStruct((number, verts, width), BF),
            jax.ShapeDtypeStruct((number, edges, width), BF),
            jax.ShapeDtypeStruct((number, wanted, width), BF),
        ]
        aliases = {}
    work = number * edges * width * width * 2 * 11
    return pl.pallas_call(
        functools.partial(step_kernel, last),
        out_shape=shapes,
        grid_spec=pltpu.PrefetchScalarGridSpec(
            num_scalar_prefetch=4,
            grid=(number,),
            in_specs=in_specs,
            out_specs=out_specs,
            scratch_shapes=[
                pltpu.VMEM((verts * 2 + gy_rows.shape[1] * 2, width), BF),
                pltpu.VMEM((verts, width), F32),
            ],
        ),
        input_output_aliases=aliases,
        cost_estimate=pl.CostEstimate(
            flops=work * 4, bytes_accessed=number * edges * width * 4, transcendentals=0
        ),
    )(inp, ids, outs, counts, *operands)


def ring(devices, by):
    return [(i, (i + by) % devices) for i in range(devices)]


def local(vertex_state, edge_state, senders, receivers, counts, border_rows, old_neighbours,
          new_neighbours, new_place, weights_in, weights_out, biases, norm_gains):
    patches, verts, width = vertex_state.shape
    edges = edge_state.shape[1]
    border = border_rows.shape[2]
    size_y = lax.axis_size("gy")
    size_x = lax.axis_size("gx")
    steps = weights_in.shape[0]
    me = lax.axis_index("gy")
    away = (new_place // patches - me) % size_y
    slot = new_place % patches
    local_ids = jnp.arange(patches, dtype=jnp.int32)
    rank = jnp.sum((away[:, None] > away[None, :]).astype(jnp.int32), axis=1)
    placed = rank[None, :] == local_ids[:, None]

    def ranked(values):
        return jnp.sum(jnp.where(placed, values[None, :], 0), axis=1)

    order, slot, counts, away = ranked(local_ids), ranked(slot), ranked(counts), ranked(away)
    lists = (
        senders.reshape(patches, 1, edges),
        receivers.reshape(patches, 1, edges),
        border_rows.reshape(patches, 1, 2 * border),
    )

    def weights_of(step):
        return weights_in[step], weights_out[step], biases[step], norm_gains[step]

    def exchange(rows):
        return (
            lax.ppermute(rows[:, :border], "gy", ring(size_y, 1)),
            lax.ppermute(rows[:, border:], "gx", ring(size_x, 1)),
        )

    first_rows = run_borders(order, vertex_state, lists[2])
    direct = size_y == patches
    finals = ()

    class Group:
        pass

    def settled(tracks):
        group = Group()
        spots = jnp.array(tracks, jnp.int32)
        lo = tracks[0]
        group.ids = order[lo : lo + len(tracks)]
        group.inp = group.ids
        group.counts = counts[lo : lo + len(tracks)]
        group.v, group.e, group.lists = vertex_state, edge_state, lists
        group.ghosts = exchange(first_rows[lo : lo + len(tracks)])
        group.near = jnp.arange(len(tracks), dtype=jnp.int32)
        return group

    def moved(tracks):
        group = Group()
        vs, es, ids, gys, gxs = [], [], [], [], []
        for track in tracks:
            spot = order[track]
            v = lax.dynamic_index_in_dim(vertex_state, spot, 0)
            e = lax.dynamic_index_in_dim(edge_state, spot, 0)
            row = jnp.concatenate(
                [lax.dynamic_index_in_dim(a, spot, 0)[:, 0] for a in lists]
                + [jnp.broadcast_to(counts[track], (1, 64)), jnp.broadcast_to(slot[track], (1, 64))],
                axis=1,
            )
            rows = first_rows[track : track + 1]
            if track:
                v, e, row = (lax.ppermute(a, "gy", ring(size_y, track)) for a in (v, e, row))
            both = [
                (x * size_y + y, (x + 1) % size_x * size_y + (y + track) % size_y)
                for x in range(size_x)
                for y in range(size_y)
            ]
            gys.append(lax.ppermute(rows[:, :border], "gy", ring(size_y, track + 1)) if (track + 1) % size_y else rows[:, :border])
            gxs.append(lax.ppermute(rows[:, border:], ("gx", "gy"), both))
            vs.append(v)
            es.append(e)
            ids.append(row)
        group.v = jnp.concatenate(vs)
        group.e = jnp.concatenate(es)
        row = jnp.concatenate(ids)
        group.ghosts = (jnp.concatenate(gys), jnp.concatenate(gxs))
        group.lists = tuple(
            row[:, None, a:b]
            for a, b in ((0, edges), (edges, 2 * edges), (2 * edges, 2 * edges + 2 * border))
        )
        end = 2 * edges + 2 * border
        group.counts = row[:, end]
        group.slots = row[:, end + 64]
        group.near = jnp.arange(len(tracks), dtype=jnp.int32)
        group.inp = group.ids = group.near
        return group

    def advance(group, step, finals=None):
        outs = group.near if finals is None else group.slots
        got = run_step(weights_of(step), group.inp, group.ids, outs, group.counts, group.v, group.e,
                       group.lists, *group.ghosts, patches, finals=finals)
        if finals is not None:
            return got
        group.v, group.e, rows = got
        group.inp = group.near
        if step < steps - 1:
            group.ghosts = exchange(rows)

    if direct:
        half = patches // 2
        far = [t for t in range(patches // 4, patches // 4 + half)]
        near = [t for t in range(patches) if t not in far]
        sets = [far[: half // 2], far[half // 2 :]]
        late = [near[: half // 2], near[half // 2 :]]
        landing = {t: lax.ppermute(jnp.broadcast_to(slot[t], (1, 128)), "gy", ring(size_y, t)) for t in far}
        late_groups = [moved(tracks) for tracks in late]
        early = [settled(tracks) for tracks in sets]
        for step in range(steps):
            for group in early:
                advance(group, step)
        arrivals = []
        for group, tracks in zip(early, sets):
            for i, track in enumerate(tracks):
                arrivals.append((
                    landing[track][0, 0],
                    lax.ppermute(group.v[i : i + 1], "gy", ring(size_y, track)),
                    lax.ppermute(group.e[i : i + 1], "gy", ring(size_y, track)),
                ))
        for step in range(steps - 1):
            for group in late_groups:
                advance(group, step)
        for group in late_groups:
            finals = advance(group, steps - 1, finals)
        vertex_out, edge_out = finals
        for where, v, e in arrivals:
            vertex_out = lax.dynamic_update_slice(vertex_out, v, (where, 0, 0))
            edge_out = lax.dynamic_update_slice(edge_out, e, (where, 0, 0))
        return vertex_out, edge_out

    half = patches // 2
    groups = [settled(list(range(half))), settled(list(range(half, patches)))]
    for step in range(steps):
        for group in groups:
            advance(group, step)
    vertex_state = jnp.concatenate([g.v for g in groups])
    edge_state = jnp.concatenate([g.e for g in groups])
    capacity = (patches + size_y - 1) // size_y
    target = (away + me) % size_y
    earlier = (target[:, None] == target[None, :]) & (local_ids[:, None] > local_ids[None, :])
    place = target * capacity + jnp.sum(earlier.astype(jnp.int32), axis=1)
    box = jnp.arange(size_y * capacity, dtype=jnp.int32)
    filled = place[None, :] == box[:, None]
    source = jnp.sum(jnp.where(filled, local_ids[None, :], 0), axis=1)
    header = jnp.where(jnp.any(filled, axis=1), slot[source], -1)
    header = jnp.broadcast_to(header[:, None], (box.shape[0], 2))
    arrived = [
        lax.all_to_all(a, "gy", split_axis=0, concat_axis=0, tiled=True)
        for a in (vertex_state[source], edge_state[source], header)
    ]
    landing = arrived[2][:, 0]
    chosen = jnp.sum(jnp.where(landing[None, :] == local_ids[:, None], box[None, :], 0), axis=1)
    return arrived[0][chosen], arrived[1][chosen]


def solution(mesh):
    held = P(("gx", "gy"))
    return jax.shard_map(
        local,
        mesh=mesh,
        in_specs=(held,) * 9 + (P(),) * 4,
        out_specs=(held, held),
        check_vma=False,
    )
```

```python
import functools

import jax
import jax.numpy as jnp
from jax import lax
from jax.experimental import pallas as pl
from jax.experimental.pallas import tpu as pltpu
from jax.sharding import PartitionSpec as P

BF = jnp.bfloat16
F32 = jnp.float32
TAIL = 16


def product(left, right):
    return jnp.dot(left, right, preferred_element_type=F32)


def ones_where(mask):
    return jnp.where(mask, jnp.ones((), BF), jnp.zeros((), BF))


def spread_ids(row):
    return jnp.transpose(jnp.broadcast_to(row, (128, row.shape[1])))


def small_ints(values):
    return values.astype(F32).astype(BF)


def one_hot(wide, number, first=0):
    lanes = lax.broadcasted_iota(jnp.int32, (1, 128), 1)
    return [
        ones_where(wide == small_ints(lanes + (first + start))) for start in range(0, number, 128)
    ]


def pick_rows(row_ids, vertices):
    wide = spread_ids(small_ints(row_ids))
    hot = jnp.concatenate(one_hot(wide, vertices.shape[0]), axis=1)
    return product(hot, vertices).astype(BF)


def updated(hidden, weights, shift, gain, after):
    width = weights.shape[1]
    wide = weights.astype(F32)
    means = jnp.broadcast_to(jnp.mean(wide, axis=1, keepdims=True), wide.shape).astype(BF)
    both = product(hidden, jnp.concatenate([weights, means], axis=1))
    center = both[:, :width] - both[:, width:] + (shift - jnp.mean(shift, axis=1, keepdims=True))
    spread = jnp.mean(center * center, axis=-1, keepdims=True)
    return center * lax.rsqrt(spread + 1e-05) * gain + after


def border_kernel(table, v_ref, b_ref, gy_ref, gx_ref):
    gy_ref[0] = pick_rows(b_ref[0, 0:1, :], v_ref[0])
    gx_ref[0] = pick_rows(b_ref[0, 1:2, :], v_ref[0])


def step_kernel(last, low, table, v_ref, e_ref, s_ref, r_ref, b_ref, gy_ref, gx_ref,
                win, wout, bias, gain, after, *rest):
    if last:
        out_ref, terms, tall = rest
    else:
        vo_ref, eo_ref, go_ref, xo_ref, terms, tall = rest
    verts = v_ref.shape[1]
    edges = e_ref.shape[1]
    border = gy_ref.shape[1]
    senders_all = verts + 2 * border
    half = senders_all // 2
    track = low + pl.program_id(0)
    spot = table[0, track]
    count = table[2, track]
    vertices = v_ref[0]
    edge = e_ref[0]
    terms[pl.ds(0, verts)] = product(vertices, win[1]).astype(BF)
    terms[pl.ds(verts, border)] = product(gy_ref[0], win[1]).astype(BF)
    terms[pl.ds(verts + border, border)] = product(gx_ref[0], win[1]).astype(BF)
    terms[pl.ds(senders_all, verts)] = product(vertices, win[2]).astype(BF)
    tall[...] = small_ints(lax.broadcasted_iota(jnp.int32, (verts, 128), 0))

    sent = small_ints(s_ref[pl.ds(spot, 1), :] - half)
    lane = lax.broadcasted_iota(jnp.int32, (1, edges), 1)
    recv = small_ints(jnp.where(lane < count, r_ref[pl.ds(spot, 1), :], -1))
    hot = jnp.concatenate(
        one_hot(spread_ids(sent), senders_all, -half) + one_hot(spread_ids(recv), verts), axis=1
    )
    summed = product(edge, win[0]) + product(hot, terms[...]) + bias[0:1, :]
    hidden = jnp.maximum(summed, 0.0).astype(BF)
    update = updated(hidden, wout[0], bias[1:2, :], gain[0:1, :], bias[2:3, :])
    row = lax.broadcasted_iota(jnp.int32, edge.shape, 0)
    widened = edge.astype(F32)
    fresh_edges = jnp.where(row < count, widened + update, widened).astype(BF)
    if last:
        out_ref[0, pl.ds(verts, edges), :] = fresh_edges
    else:
        eo_ref[0] = fresh_edges
    column = tall[...]
    incoming = jnp.concatenate(
        [ones_where(column == recv[:, k : k + 128]) for k in range(0, edges, 128)], axis=1
    )
    aggregate = product(incoming, fresh_edges).astype(BF)

    hidden = product(vertices, win[3]) + product(aggregate, win[4]) + bias[3:4, :]
    hidden = jnp.maximum(hidden, 0.0).astype(BF)
    update = updated(hidden, wout[1], bias[4:5, :], gain[1:2, :], bias[5:6, :])
    fresh = (vertices.astype(F32) + update).astype(BF)
    if last:
        out_ref[0, pl.ds(0, verts), :] = fresh
        slot = jnp.full((TAIL, fresh.shape[1]), table[1, track], jnp.int32)
        out_ref[0, pl.ds(verts + edges, TAIL), :] = small_ints(slot)
    else:
        vo_ref[0] = fresh
        go_ref[0] = pick_rows(b_ref[0, 0:1, :], fresh)
        xo_ref[0] = pick_rows(b_ref[0, 1:2, :], fresh)


def run_borders(table, vertex_state, border_rows):
    patches, verts, width = vertex_state.shape
    border = border_rows.shape[2]
    return pl.pallas_call(
        border_kernel,
        out_shape=[jax.ShapeDtypeStruct((patches, border, width), BF)] * 2,
        grid_spec=pltpu.PrefetchScalarGridSpec(
            num_scalar_prefetch=1,
            grid=(patches,),
            in_specs=[
                pl.BlockSpec((1, verts, width), lambda p, t: (t[0, p], 0, 0)),
                pl.BlockSpec((1, 2, border), lambda p, t: (t[0, p], 0, 0)),
            ],
            out_specs=[pl.BlockSpec((1, border, width), lambda p, t: (p, 0, 0))] * 2,
        ),
        name="borders",
    )(table, vertex_state, border_rows)


def run_step(weights, step, table, low, number, state, state_at, lists, ghosts, ghosts_at, after, last):
    v, e = state
    senders, receivers, border_rows = lists
    verts, width = v.shape[1:]
    edges = e.shape[1]
    border = border_rows.shape[2]

    def listed(p, t):
        return (t[0, low + p], 0, 0)

    def shifted(by):
        return lambda p, t: (p + by, 0, 0)

    def whole(array):
        return pl.BlockSpec(array.shape, lambda p, t: (0,) * array.ndim)

    def of_step(array):
        return pl.BlockSpec((None,) + array.shape[1:], lambda p, t: (step,) + (0,) * (array.ndim - 1))

    state_map = listed if state_at is None else shifted(state_at)
    in_specs = [
        pl.BlockSpec((1, verts, width), state_map),
        pl.BlockSpec((1, edges, width), state_map),
        whole(senders),
        whole(receivers),
        pl.BlockSpec((1, 2, border), listed),
        pl.BlockSpec((1, border, width), shifted(ghosts_at)),
        pl.BlockSpec((1, border, width), shifted(ghosts_at)),
        *[of_step(array) for array in weights],
        pl.BlockSpec(memory_space=pl.ANY),
    ]
    rows = [verts + edges + TAIL] if last else [verts, edges, border, border]
    work = number * edges * width * width * 2 * 11
    return pl.pallas_call(
        functools.partial(step_kernel, last, low),
        out_shape=[jax.ShapeDtypeStruct((number, r, width), BF) for r in rows],
        grid_spec=pltpu.PrefetchScalarGridSpec(
            num_scalar_prefetch=1,
            grid=(number,),
            in_specs=in_specs,
            out_specs=[pl.BlockSpec((1, r, width), lambda p, t: (p, 0, 0)) for r in rows],
            scratch_shapes=[
                pltpu.VMEM((verts * 2 + border * 2, width), BF),
                pltpu.VMEM((verts, 128), BF),
            ],
        ),
        cost_estimate=pl.CostEstimate(
            flops=work * 4, bytes_accessed=number * edges * width * 4, transcendentals=0
        ),
        name="step",
    )(table, v, e, senders, receivers, border_rows, *ghosts, *weights, after)


def landing_kernel(number, verts, edges, where, *refs):
    packed = refs[:number]
    vo_ref, eo_ref, held, in_sem, out_sem = refs[number:]
    inward = [
        pltpu.make_async_copy(packed[t].at[0], held.at[t], in_sem.at[t]) for t in range(number)
    ]
    for copy in inward:
        copy.start()
    outward = []
    for t in range(number):
        inward[t].wait()
        parts = (
            pltpu.make_async_copy(held.at[t, pl.ds(0, verts)], vo_ref.at[where[t]], out_sem.at[0, t]),
            pltpu.make_async_copy(held.at[t, pl.ds(verts, edges)], eo_ref.at[where[t]], out_sem.at[1, t]),
        )
        for copy in parts:
            copy.start()
        outward += parts
    for copy in outward:
        copy.wait()


def land(where, packed, verts, edges):
    number = len(packed)
    width = packed[0].shape[2]
    anywhere = pl.BlockSpec(memory_space=pl.ANY)
    return pl.pallas_call(
        functools.partial(landing_kernel, number, verts, edges),
        out_shape=[
            jax.ShapeDtypeStruct((number, verts, width), BF),
            jax.ShapeDtypeStruct((number, edges, width), BF),
        ],
        grid_spec=pltpu.PrefetchScalarGridSpec(
            num_scalar_prefetch=1,
            grid=(),
            in_specs=[anywhere] * number,
            out_specs=[anywhere] * 2,
            scratch_shapes=[
                pltpu.VMEM((number,) + packed[0].shape[1:], BF),
                pltpu.SemaphoreType.DMA((number,)),
                pltpu.SemaphoreType.DMA((2, number)),
            ],
        ),
        name="land",
    )(where, *packed)


def ring(devices, by):
    return [(i, (i + by) % devices) for i in range(devices)]


class Group:
    pass


def local(vertex_state, edge_state, senders, receivers, counts, border_rows, old_neighbours,
          new_neighbours, new_place, *weights):
    patches, verts, width = vertex_state.shape
    edges = edge_state.shape[1]
    size_y = lax.axis_size("gy")
    size_x = lax.axis_size("gx")
    steps = weights[0].shape[0]
    me = lax.axis_index("gy")
    direct = size_y == patches
    away = (new_place // patches - me) % size_y
    if direct:
        near = jnp.minimum(away, size_y - away)
        key = (size_y - near) * 2 + (away > size_y // 2)
        sequence = sorted(range(size_y), key=lambda t: (size_y - min(t, size_y - t)) * 2 + (t > size_y // 2))
    else:
        key = away
    local_ids = jnp.arange(patches, dtype=jnp.int32)
    rank = jnp.sum((key[:, None] > key[None, :]).astype(jnp.int32), axis=1)
    placed = rank[None, :] == local_ids[:, None]
    known = jnp.stack([local_ids, new_place % patches, counts, away])
    table = jnp.sum(jnp.where(placed[None], known[:, None, :], 0), axis=2)
    lists = (senders, receivers, border_rows)

    def exchange(gy_rows, gx_rows):
        return (
            lax.ppermute(gy_rows, "gy", ring(size_y, 1)),
            lax.ppermute(gx_rows, "gx", ring(size_x, 1)),
        )

    picked = run_borders(table, vertex_state, border_rows)
    first_ghosts = exchange(*picked)
    latest = [picked[0]]

    def group_of(low, high):
        group = Group()
        group.low, group.number = low, high - low
        group.state, group.at = (vertex_state, edge_state), None
        group.ghosts, group.ghosts_at = first_ghosts, low
        group.step = 0
        return group

    arrived = [None] * patches

    def send(track, packed):
        if direct and sequence[track]:
            packed = lax.ppermute(packed, "gy", ring(size_y, sequence[track]))
        arrived[track] = packed

    def advance(group):
        if group.step < steps - 1:
            v, e, *rows = run_step(weights, group.step, table, group.low, group.number, group.state,
                                   group.at, lists, group.ghosts, group.ghosts_at, latest[0], False)
            latest[0] = rows[0]
            group.state, group.at = (v, e), 0
            group.ghosts, group.ghosts_at = exchange(*rows), 0
        else:
            for i in range(group.number):
                (packed,) = run_step(
                    weights, group.step, table, group.low + i, 1, group.state,
                    None if group.at is None else group.at + i, lists, group.ghosts,
                    group.ghosts_at + i, latest[0], True)
                latest[0] = packed
                send(group.low + i, packed)
        group.step += 1

    cuts = [0, (3 * patches + 7) // 8, (6 * patches + 7) // 8, patches]
    a, b, c = (group_of(low, high) for low, high in zip(cuts[:-1], cuts[1:]))
    for _ in range(steps - 1):
        advance(a)
        advance(b)
    advance(a)
    advance(c)
    advance(b)
    for _ in range(steps - 1):
        advance(c)

    if direct:
        where = jnp.stack([packed[0, verts + edges, 0] for packed in arrived]).astype(jnp.int32)
        return tuple(land(where, arrived, verts, edges))

    packed = jnp.concatenate(arrived)
    slot, away = table[1], table[3]
    capacity = (patches + size_y - 1) // size_y
    target = (away + me) % size_y
    earlier = (target[:, None] == target[None, :]) & (local_ids[:, None] > local_ids[None, :])
    place = target * capacity + jnp.sum(earlier.astype(jnp.int32), axis=1)
    box = jnp.arange(size_y * capacity, dtype=jnp.int32)
    filled = place[None, :] == box[:, None]
    source = jnp.sum(jnp.where(filled, local_ids[None, :], 0), axis=1)
    header = jnp.where(jnp.any(filled, axis=1), slot[source], -1)
    header = jnp.broadcast_to(header[:, None], (box.shape[0], 2))
    packed, header = [
        lax.all_to_all(array, "gy", split_axis=0, concat_axis=0, tiled=True)
        for array in (packed[source], header)
    ]
    landing = header[:, 0]
    chosen = jnp.sum(jnp.where(landing[None, :] == local_ids[:, None], box[None, :], 0), axis=1)
    packed = packed[chosen]
    return packed[:, :verts], packed[:, verts : verts + edges]


def solution(mesh):
    held = P(("gx", "gy"))
    return jax.shard_map(
        local,
        mesh=mesh,
        in_specs=(held,) * 9 + (P(),) * 4,
        out_specs=(held, held),
        check_vma=False,
    )
```

```python
import functools

import jax
import jax.numpy as jnp
from jax import lax
from jax.experimental import pallas as pl
from jax.experimental.pallas import tpu as pltpu
from jax.sharding import PartitionSpec as P


BF = jnp.bfloat16
F32 = jnp.float32
TAIL = 16


def product(left, right):
    return jnp.dot(left, right, preferred_element_type=F32)


def ones_where(mask):
    return jnp.where(mask, jnp.ones((), BF), jnp.zeros((), BF))


def spread_ids(row):
    return jnp.transpose(jnp.broadcast_to(row, (128, row.shape[1])))


def small_ints(values):
    return values.astype(F32).astype(BF)


def one_hot(wide, number, first=0):
    lanes = lax.broadcasted_iota(jnp.int32, (1, 128), 1)
    return [
        ones_where(wide == small_ints(lanes + (first + start))) for start in range(0, number, 128)
    ]


def pick_rows(row_ids, vertices):
    wide = spread_ids(small_ints(row_ids))
    hot = jnp.concatenate(one_hot(wide, vertices.shape[0]), axis=1)
    return product(hot, vertices).astype(BF)


def updated(hidden, weights, shift, gain, after):
    width = weights.shape[1]
    wide = weights.astype(F32)
    means = jnp.broadcast_to(jnp.mean(wide, axis=1, keepdims=True), wide.shape).astype(BF)
    both = product(hidden, jnp.concatenate([weights, means], axis=1))
    center = both[:, :width] - both[:, width:] + (shift - jnp.mean(shift, axis=1, keepdims=True))
    spread = jnp.mean(center * center, axis=-1, keepdims=True)
    return center * lax.rsqrt(spread + 1e-05) * gain + after


def border_kernel(table, v_ref, b_ref, gy_ref, gx_ref):
    gy_ref[0] = pick_rows(b_ref[0, 0:1, :], v_ref[0])
    gx_ref[0] = pick_rows(b_ref[0, 1:2, :], v_ref[0])


def step_kernel(last, low, table, v_ref, e_ref, s_ref, r_ref, b_ref, gy_ref, gx_ref,
                win, wout, bias, gain, after, *rest):
    if last:
        out_ref, terms, tall = rest
    else:
        vo_ref, eo_ref, go_ref, xo_ref, terms, tall = rest
    verts = v_ref.shape[1]
    edges = e_ref.shape[1]
    border = gy_ref.shape[1]
    senders_all = verts + 2 * border
    half = senders_all // 2
    track = low + pl.program_id(0)
    spot = table[0, track]
    count = table[2, track]
    vertices = v_ref[0]
    edge = e_ref[0]
    terms[pl.ds(0, verts)] = product(vertices, win[1]).astype(BF)
    terms[pl.ds(verts, border)] = product(gy_ref[0], win[1]).astype(BF)
    terms[pl.ds(verts + border, border)] = product(gx_ref[0], win[1]).astype(BF)
    terms[pl.ds(senders_all, verts)] = product(vertices, win[2]).astype(BF)
    tall[...] = small_ints(lax.broadcasted_iota(jnp.int32, (verts, 128), 0))

    sent = small_ints(s_ref[pl.ds(spot, 1), :] - half)
    lane = lax.broadcasted_iota(jnp.int32, (1, edges), 1)
    recv = small_ints(jnp.where(lane < count, r_ref[pl.ds(spot, 1), :], -1))
    hot = jnp.concatenate(
        one_hot(spread_ids(sent), senders_all, -half) + one_hot(spread_ids(recv), verts), axis=1
    )
    summed = product(edge, win[0]) + product(hot, terms[...]) + bias[0:1, :]
    hidden = jnp.maximum(summed, 0.0).astype(BF)
    update = updated(hidden, wout[0], bias[1:2, :], gain[0:1, :], bias[2:3, :])
    row = lax.broadcasted_iota(jnp.int32, edge.shape, 0)
    widened = edge.astype(F32)
    fresh_edges = jnp.where(row < count, widened + update, widened).astype(BF)
    if last:
        out_ref[0, pl.ds(verts, edges), :] = fresh_edges
    else:
        eo_ref[0] = fresh_edges
    column = tall[...]
    incoming = jnp.concatenate(
        [ones_where(column == recv[:, k : k + 128]) for k in range(0, edges, 128)], axis=1
    )
    aggregate = product(incoming, fresh_edges).astype(BF)

    hidden = product(vertices, win[3]) + product(aggregate, win[4]) + bias[3:4, :]
    hidden = jnp.maximum(hidden, 0.0).astype(BF)
    update = updated(hidden, wout[1], bias[4:5, :], gain[1:2, :], bias[5:6, :])
    fresh = (vertices.astype(F32) + update).astype(BF)
    if last:
        out_ref[0, pl.ds(0, verts), :] = fresh
        slot = jnp.full((TAIL, fresh.shape[1]), table[1, track], jnp.int32)
        out_ref[0, pl.ds(verts + edges, TAIL), :] = small_ints(slot)
    else:
        vo_ref[0] = fresh
        go_ref[0] = pick_rows(b_ref[0, 0:1, :], fresh)
        xo_ref[0] = pick_rows(b_ref[0, 1:2, :], fresh)


def run_borders(table, vertex_state, border_rows):
    patches, verts, width = vertex_state.shape
    border = border_rows.shape[2]
    return pl.pallas_call(
        border_kernel,
        out_shape=[jax.ShapeDtypeStruct((patches, border, width), BF)] * 2,
        grid_spec=pltpu.PrefetchScalarGridSpec(
            num_scalar_prefetch=1,
            grid=(patches,),
            in_specs=[
                pl.BlockSpec((1, verts, width), lambda p, t: (t[0, p], 0, 0)),
                pl.BlockSpec((1, 2, border), lambda p, t: (t[0, p], 0, 0)),
            ],
            out_specs=[pl.BlockSpec((1, border, width), lambda p, t: (p, 0, 0))] * 2,
        ),
        name="borders",
    )(table, vertex_state, border_rows)


def run_step(weights, step, table, low, number, state, state_at, lists, ghosts, ghosts_at, after, last):
    v, e = state
    senders, receivers, border_rows = lists
    verts, width = v.shape[1:]
    edges = e.shape[1]
    border = border_rows.shape[2]

    def listed(p, t):
        return (t[0, low + p], 0, 0)

    def shifted(by):
        return lambda p, t: (p + by, 0, 0)

    def whole(array):
        return pl.BlockSpec(array.shape, lambda p, t: (0,) * array.ndim)

    def of_step(array):
        return pl.BlockSpec((None,) + array.shape[1:], lambda p, t: (step,) + (0,) * (array.ndim - 1))

    state_map = listed if state_at is None else shifted(state_at)
    in_specs = [
        pl.BlockSpec((1, verts, width), state_map),
        pl.BlockSpec((1, edges, width), state_map),
        whole(senders),
        whole(receivers),
        pl.BlockSpec((1, 2, border), listed),
        pl.BlockSpec((1, border, width), shifted(ghosts_at)),
        pl.BlockSpec((1, border, width), shifted(ghosts_at)),
        *[of_step(array) for array in weights],
        pl.BlockSpec(memory_space=pl.ANY),
    ]
    rows = [verts + edges + TAIL] if last else [verts, edges, border, border]
    work = number * edges * width * width * 2 * 11
    return pl.pallas_call(
        functools.partial(step_kernel, last, low),
        out_shape=[jax.ShapeDtypeStruct((number, r, width), BF) for r in rows],
        grid_spec=pltpu.PrefetchScalarGridSpec(
            num_scalar_prefetch=1,
            grid=(number,),
            in_specs=in_specs,
            out_specs=[pl.BlockSpec((1, r, width), lambda p, t: (p, 0, 0)) for r in rows],
            scratch_shapes=[
                pltpu.VMEM((verts * 2 + border * 2, width), BF),
                pltpu.VMEM((verts, 128), BF),
            ],
        ),
        cost_estimate=pl.CostEstimate(
            flops=work // 64, bytes_accessed=number * edges * width // 64, transcendentals=0
        ),
        name="step",
    )(table, v, e, senders, receivers, border_rows, *ghosts, *weights, after)


def landing_kernel(spots, verts, edges, *refs):
    number = len(spots)
    packed = refs[:number]
    vo_ref, eo_ref, held, in_sem, out_sem = refs[number:]
    inward = [
        pltpu.make_async_copy(packed[t].at[spots[t]], held.at[t], in_sem.at[t])
        for t in range(number)
    ]
    for copy in inward:
        copy.start()
    outward = []
    for t in range(number):
        inward[t].wait()
        slot = jnp.max(held[t, pl.ds(verts + edges, TAIL), :].astype(F32)).astype(jnp.int32)
        parts = (
            pltpu.make_async_copy(held.at[t, pl.ds(0, verts)], vo_ref.at[slot], out_sem.at[0, t]),
            pltpu.make_async_copy(held.at[t, pl.ds(verts, edges)], eo_ref.at[slot], out_sem.at[1, t]),
        )
        for copy in parts:
            copy.start()
        outward += parts
    for copy in outward:
        copy.wait()


def land(packed, spots, verts, edges):
    number = len(packed)
    width = packed[0].shape[2]
    anywhere = pl.BlockSpec(memory_space=pl.ANY)
    return pl.pallas_call(
        functools.partial(landing_kernel, spots, verts, edges),
        out_shape=[
            jax.ShapeDtypeStruct((number, verts, width), BF),
            jax.ShapeDtypeStruct((number, edges, width), BF),
        ],
        in_specs=[anywhere] * number,
        out_specs=[anywhere] * 2,
        scratch_shapes=[
            pltpu.VMEM((number,) + packed[0].shape[1:], BF),
            pltpu.SemaphoreType.DMA((number,)),
            pltpu.SemaphoreType.DMA((2, number)),
        ],
        name="land",
    )(*packed)


def ring(devices, by):
    return [(i, (i + by) % devices) for i in range(devices)]


class Group:
    pass


def local(vertex_state, edge_state, senders, receivers, counts, border_rows, old_neighbours,
          new_neighbours, new_place, *weights):
    patches, verts, _ = vertex_state.shape
    edges = edge_state.shape[1]
    size_y = lax.axis_size("gy")
    size_x = lax.axis_size("gx")
    steps = weights[0].shape[0]
    me = lax.axis_index("gy")
    direct = size_y == patches
    away = (new_place // patches - me) % size_y
    if direct:
        near = jnp.minimum(away, size_y - away)
        key = (size_y - near) * 2 + (away > size_y // 2)
        sequence = sorted(range(size_y), key=lambda t: (size_y - min(t, size_y - t)) * 2 + (t > size_y // 2))
    else:
        key = away
    local_ids = jnp.arange(patches, dtype=jnp.int32)
    rank = jnp.sum((key[:, None] > key[None, :]).astype(jnp.int32), axis=1)
    placed = rank[None, :] == local_ids[:, None]
    known = jnp.stack([local_ids, new_place % patches, counts, away])
    table = jnp.sum(jnp.where(placed[None], known[:, None, :], 0), axis=2)
    lists = (senders, receivers, border_rows)

    def exchange(gy_rows, gx_rows):
        return (
            lax.ppermute(gy_rows, "gy", ring(size_y, 1)),
            lax.ppermute(gx_rows, "gx", ring(size_x, 1)),
        )

    picked = run_borders(table, vertex_state, border_rows)
    first_ghosts = exchange(*picked)
    latest = [picked[0]]

    def group_of(low, high):
        group = Group()
        group.low, group.number = low, high - low
        group.state, group.at = (vertex_state, edge_state), None
        group.ghosts, group.ghosts_at = first_ghosts, low
        group.step = 0
        return group

    arrived = [None] * patches
    spots = [0] * patches
    ended = []

    def send(track, packed, spot):
        if sequence[track]:
            packed = packed[spot : spot + 1]
            packed = lax.ppermute(packed, "gy", ring(size_y, sequence[track]))
            spot = 0
        arrived[track], spots[track] = packed, spot

    done = []

    def advance(group):
        done.append(group)
        if group.step < steps - 1:
            v, e, *rows = run_step(weights, group.step, table, group.low, group.number, group.state,
                                   group.at, lists, group.ghosts, group.ghosts_at, latest[0], False)
            latest[0] = rows[0]
            group.state, group.at = (v, e), 0
            group.ghosts, group.ghosts_at = exchange(*rows), 0
        else:
            (packed,) = run_step(weights, group.step, table, group.low, group.number, group.state,
                                 group.at, lists, group.ghosts, group.ghosts_at, latest[0], True)
            latest[0] = packed
            if direct:
                for i in range(group.number):
                    send(group.low + i, packed, i)
            else:
                ended.append((group.low, packed))
        group.step += 1

    cuts = [0, (3 * patches + 7) // 8, (6 * patches + 7) // 8, patches]
    a, b, c = (group_of(low, high) for low, high in zip(cuts[:-1], cuts[1:]))
    turns = [a, b] * 1 + [x for _ in range(steps - 2) for x in (a, c)] + [a]
    left = {b: steps - turns.count(b), c: steps - turns.count(c)}
    while left[b] or left[c]:
        for group in (b, c):
            if left[group]:
                turns.append(group)
                left[group] -= 1
    for group in turns:
        advance(group)

    if direct:
        return tuple(land(arrived, spots, verts, edges))

    packed = jnp.concatenate([part for _, part in sorted(ended, key=lambda pair: pair[0])])
    slot, away = table[1], table[3]
    capacity = (patches + size_y - 1) // size_y
    target = (away + me) % size_y
    earlier = (target[:, None] == target[None, :]) & (local_ids[:, None] > local_ids[None, :])
    place = target * capacity + jnp.sum(earlier.astype(jnp.int32), axis=1)
    box = jnp.arange(size_y * capacity, dtype=jnp.int32)
    filled = place[None, :] == box[:, None]
    source = jnp.sum(jnp.where(filled, local_ids[None, :], 0), axis=1)
    header = jnp.where(jnp.any(filled, axis=1), slot[source], -1)
    header = jnp.broadcast_to(header[:, None], (box.shape[0], 2))
    packed, header = [
        lax.all_to_all(array, "gy", split_axis=0, concat_axis=0, tiled=True)
        for array in (packed[source], header)
    ]
    landing = header[:, 0]
    chosen = jnp.sum(jnp.where(landing[None, :] == local_ids[:, None], box[None, :], 0), axis=1)
    packed = packed[chosen]
    return packed[:, :verts], packed[:, verts : verts + edges]


def solution(mesh):
    held = P(("gx", "gy"))

    return jax.shard_map(
        local,
        mesh=mesh,
        in_specs=(held,) * 9 + (P(),) * 4,
        out_specs=(held, held),
        check_vma=False,
    )
```
